32 devices in a mesh: grp: 2 (over x), px: 4 (over y, core), py: 4 (over z).
Axes of the slice: x: 2, y: 2, z: 4, core: 2. Of those that a mesh axis runs over, the one named last changes fastest.
Arguments:
- multiplier: float32 [3, 32, 16, 256, 256], P(None, 'py', None, ('grp', 'px')), may hold values from -6 to 6
- auxiliary: float32 [3, 32, 16, 256, 256], P(None, 'py', None, ('grp', 'px')), may hold values from -6 to 6
- density_start: float32 [16, 256, 256], P(None, ('grp', 'px')), may hold values from 0.5 to 2
- density_end: float32 [16, 256, 256], P(None, ('grp', 'px')), may hold values from 0.5 to 2
Outputs:
- multiplier_next: float32 [3, 32, 16, 256, 256], P(None, 'py', None, ('grp', 'px'))
- auxiliary_next: float32 [3, 32, 16, 256, 256], P(None, 'py', None, ('grp', 'px'))
The draws below stay inside these ranges and needn't reach their ends.
All inputs are finite; a program needn't handle non-finite values.
Results may differ from the reference program's by a relative error of at most 0.0003.
Values sent between devices are 32-bit elements; how exact they have to be, the bound alone decides.
A program may use at most 128 MiB of HBM per device.

```python
import math
import jax
import jax.numpy as jnp
from jax import lax

NX = 256
NY = 256
LEVELS = 32
BATCH = 16
NEWTON = 4


def wave_field(key):
    keys = jax.random.split(key, 4)
    problem = jnp.arange(BATCH, dtype=jnp.int32)
    low_shift = jax.random.randint(keys[0], (), 0, 9)
    high_shift = jax.random.randint(keys[1], (), 0, 13)
    low_wave = 12 + (problem * 9 // BATCH + low_shift) % 9
    high_wave = 28 + (problem * 13 // BATCH + high_shift) % 13
    phases = jax.random.uniform(keys[2], (2, BATCH, 1, 1), jnp.float32, -math.pi, math.pi)
    row_signs = jnp.where(jax.random.bernoulli(keys[3], 0.5, (2, BATCH, NX, 1)), 1.0, -1.0).astype(jnp.float32)
    column = jnp.arange(NY, dtype=jnp.int32)
    low_phase = (low_wave[:, None] * column[None, :] % NY).astype(jnp.float32) * (2.0 * math.pi / NY)
    high_phase = (high_wave[:, None] * column[None, :] % NY).astype(jnp.float32) * (2.0 * math.pi / NY)
    low_part = jnp.cos(low_phase[:, None, :] + phases[0]) * row_signs[0]
    high_part = jnp.cos(high_phase[:, None, :] + phases[1]) * row_signs[1]
    return 1.5 * (low_part + high_part)


def field_draw(key):
    base_key = jax.random.fold_in(key, 101)
    wave_key = jax.random.fold_in(key, 202)
    shape = (3, LEVELS, BATCH, NX, NY)
    base = jax.random.normal(base_key, shape, jnp.float32)
    wave = wave_field(wave_key)
    second = base[2] + wave[None]
    whole = jnp.concatenate([base[:2], second[None]], axis=0)
    return jnp.clip(whole, -6.0, 6.0).astype(jnp.float32)


def draw_multiplier(key, part):
    return field_draw(jax.random.fold_in(key, 11))


def draw_auxiliary(key, part):
    return field_draw(jax.random.fold_in(key, 23))


def block_scale(stream_key, extent, cuts, least, high):
    def one(position, parts):
        draws = jax.random.uniform(jax.random.fold_in(jax.random.fold_in(stream_key, 6), position), (parts,), jnp.float32, least / len(cuts), high / len(cuts))
        return jnp.repeat(jnp.exp(draws), extent[position] // parts).reshape((-1,) + (1,) * (len(extent) - position - 1))

    gain = one(*cuts[0])
    for cut in cuts[1:]:
        gain = gain * one(*cut)
    return gain


def setup_inputs(seed: int = 0) -> dict:
    key_of = jax.random.split(jax.random.key(seed), 5)
    return {
        "multiplier": draw_multiplier(jax.random.fold_in(key_of[4], 71), 0),
        "auxiliary": draw_auxiliary(jax.random.fold_in(key_of[4], 71), 0),
        "density_start": jnp.clip(jnp.exp(math.log(2.0) - 1.3862944 * jax.random.uniform(key_of[2], (BATCH, NX, NY), jnp.float32) ** block_scale(key_of[2], (BATCH, NX, NY), ((1, 8),), -0.2, 0.2)), 0.5, 2.0),
        "density_end": jnp.clip(jnp.exp(math.log(2.0) - 1.3862944 * jax.random.uniform(key_of[3], (BATCH, NX, NY), jnp.float32) ** block_scale(key_of[3], (BATCH, NX, NY), ((1, 8),), -0.2, 0.2)), 0.5, 2.0),
    }


PENALTY = 1.0
PRECISE = lax.Precision.HIGHEST

def cosine_table(levels):
    mode_index = lax.broadcasted_iota(jnp.int32, (levels, levels), 0)
    time_index = lax.broadcasted_iota(jnp.int32, (levels, levels), 1)
    phase_index = mode_index * (2 * time_index + 1) % (4 * levels)
    angles = phase_index.astype(jnp.float32) * (math.pi / (2 * levels))
    weights = jnp.where(mode_index == 0, math.sqrt(1.0 / levels), math.sqrt(2.0 / levels))
    return weights * jnp.cos(angles)

def eigenvalues(levels, row_start, row_total, row_count, col_count):
    time_modes = lax.broadcasted_iota(jnp.int32, (levels, 1, 1, 1), 0).astype(jnp.float32)
    row_modes = (row_start + lax.broadcasted_iota(jnp.int32, (1, 1, row_total, 1), 2)).astype(jnp.float32)
    col_modes = lax.broadcasted_iota(jnp.int32, (1, 1, 1, col_count), 3).astype(jnp.float32)
    time_part = 4.0 * jnp.sin(time_modes * (math.pi / (2 * levels))) ** 2
    row_part = 4.0 * jnp.sin(row_modes * (math.pi / row_count)) ** 2
    col_part = 4.0 * jnp.sin(col_modes * (math.pi / col_count)) ** 2
    return time_part + row_part + col_part

def project(target):
    time_part = target[0]
    space_first = target[1]
    space_second = target[2]
    kinetic = 0.5 * (space_first * space_first + space_second * space_second)
    offset_one = 1.0 + time_part
    scaling = jnp.maximum(offset_one, 1.0) + jnp.cbrt(kinetic)
    for newton_step in range(NEWTON):
        residue = scaling * scaling * (scaling - offset_one) - kinetic
        derivative = scaling * (3.0 * scaling - 2.0 * offset_one)
        scaling = jnp.maximum(scaling - residue / derivative, 1.0)
    feasible = time_part + kinetic <= 0.0
    return jnp.stack([jnp.where(feasible, time_part, time_part - (scaling - 1.0)), jnp.where(feasible, space_first, space_first / scaling), jnp.where(feasible, space_second, space_second / scaling)])

def reference(multiplier, auxiliary, density_start, density_end):
    offset_field = auxiliary - multiplier / PENALTY
    level_index = lax.broadcasted_iota(jnp.int32, (LEVELS, 1, 1, 1), 0)
    offset_time = jnp.where(level_index == LEVELS - 1, 0.0, offset_field[0])
    earlier = jnp.concatenate([jnp.zeros_like(offset_time[:1]), offset_time[:-1]], axis=0)
    boundary = jnp.where(level_index == 0, -density_start / PENALTY, 0.0) + jnp.where(level_index == LEVELS - 1, density_end / PENALTY, 0.0)
    offset_first = offset_field[1]
    offset_second = offset_field[2]
    source = earlier - offset_time + jnp.roll(offset_first, 1, axis=2) - offset_first + jnp.roll(offset_second, 1, axis=3) - offset_second + boundary
    cosine = cosine_table(LEVELS)
    transformed = jnp.einsum('kt,tbxy->kbxy', cosine, source, precision=PRECISE)
    spectrum = jnp.fft.fft2(transformed, axes=(2, 3))
    eigen = eigenvalues(LEVELS, 0, NX, NX, NY)
    positive = eigen > 0.0
    inverse = jnp.where(positive, 1.0 / jnp.where(positive, eigen, 1.0), 0.0)
    potential_modes = jnp.real(jnp.fft.ifft2(spectrum * inverse, axes=(2, 3))).astype(source.dtype)
    potential = jnp.einsum('kt,kbxy->tbxy', cosine, potential_modes, precision=PRECISE)
    time_rate = jnp.concatenate([potential[1:] - potential[:-1], jnp.zeros_like(potential[:1])], axis=0)
    gradient = jnp.stack([time_rate, jnp.roll(potential, -1, axis=2) - potential, jnp.roll(potential, -1, axis=3) - potential])
    target = gradient + multiplier / PENALTY
    auxiliary_next = project(target)
    multiplier_next = multiplier + PENALTY * (gradient - auxiliary_next)
    return (multiplier_next, auxiliary_next)
```

```python
import functools
import math

import jax
import jax.numpy as jnp
from jax import lax
from jax.experimental import pallas as pl
from jax.experimental.pallas import tpu as pltpu
from jax.sharding import PartitionSpec as P

NEWTON = 4
PENALTY = 1.0
PRECISE = lax.Precision.HIGHEST
VMEM_LIMIT = 60 * 1024 * 1024
SPACE = ("grp", "px")


def dot(a, b):
    return jnp.dot(a, b, precision=PRECISE, preferred_element_type=jnp.float32)


def hartley_table(length):
    row_index = lax.broadcasted_iota(jnp.int32, (length, length), 0)
    col_index = lax.broadcasted_iota(jnp.int32, (length, length), 1)
    phase_index = row_index * col_index % length
    angles = phase_index.astype(jnp.float32) * (2.0 * math.pi / length)
    return (jnp.cos(angles) + jnp.sin(angles)) / math.sqrt(length)


def mode_tables(rows, cols, here, blocks, block):
    m = lax.broadcasted_iota(jnp.int32, (rows, cols), 0)
    n = lax.broadcasted_iota(jnp.int32, (rows, cols), 1)
    m = jnp.minimum(m, rows - m).astype(jnp.float32)
    n = jnp.minimum(n, cols - n).astype(jnp.float32)
    lam = 4.0 * jnp.sin(m * (math.pi / rows)) ** 2 + 4.0 * jnp.sin(n * (math.pi / cols)) ** 2
    sinh = jnp.sqrt(lam * (1.0 + 0.25 * lam))
    inverse = 1.0 + 0.5 * lam + sinh
    ratio = 1.0 / inverse
    step = lax.integer_pow(ratio, here)
    double = step * step
    low = jnp.ones_like(step)
    high = jnp.ones_like(step)
    full = double
    for k in range(1, blocks):
        low = jnp.where(block >= k, low * double, low)
        high = jnp.where(blocks - 1 - block >= k, high * double, high)
        full = full * double
    positive = lam > 0.0
    scale = jnp.where(
        positive, 0.5 / jnp.where(positive, sinh * (1.0 - full), 1.0), 0.0
    )
    return jnp.stack([ratio, inverse, low, high, scale]), step


def source_kernel(mult, aux, start, end, table, out, prev, body, tail, *, levels):
    t = pl.program_id(0)
    here = pl.num_programs(0)
    problems, rows, cols = body.shape
    group, per = out.shape[0], out.shape[1]
    level = lax.axis_index("py") * here + t
    first = level == 0
    last = level == levels - 1

    @pl.when(t == 0)
    def _():
        prev[...] = jnp.zeros_like(prev)
        tail[...] = jnp.zeros_like(tail)

    row = lax.broadcasted_iota(jnp.int32, (rows, cols), 0)
    keep = jnp.where(last, 0.0, 1.0)
    begin = jnp.where(first, -1.0 / PENALTY, 0.0)
    finish = jnp.where(last, 1.0 / PENALTY, 0.0)

    def one(b, carry):
        along = aux[1, 0, b] - mult[1, 0, b] / PENALTY
        beside = jnp.where(row == 0, 0.0, pltpu.roll(along, 1, 0))
        second = aux[2, 0, b] - mult[2, 0, b] / PENALTY
        across = pltpu.roll(second, 1, 1) - second
        now = (aux[0, 0, b] - mult[0, 0, b] / PENALTY) * keep
        boundary = begin * start[b] + finish * end[b]
        body[b] = prev[b] - now + beside - along + across + boundary
        prev[b] = now
        tail[b, pl.ds(t, 1), :] = along[rows - 1 :, :]
        return carry

    lax.fori_loop(0, problems, one, 0)
    spread = dot(body[...].reshape(problems * rows, cols), table[...])
    at = pl.multiple_of(t * rows, rows)
    out[:, :, pl.ds(at, rows), :] = spread.reshape(group, per, rows, cols)

    @pl.when(t == here - 1)
    def _():
        beyond = dot(prev[...].reshape(problems * rows, cols), table[...])
        out[:, :, here * rows : here * rows + rows, :] = beyond.reshape(group, per, rows, cols)
        held = tail.shape[1]
        rims = dot(tail[...].reshape(problems * held, cols), table[...])
        out[:, :, here * rows + rows :, :] = rims.reshape(group, per, held, cols)


def forward_kernel(x, table, coef, modes, up, down, plane, *, here, rows):
    group = x.shape[0]
    total, cols = table.shape[0], x.shape[3]

    def one(t, carry):
        at = pl.multiple_of(t * rows, rows)
        plane[...] = x[:, 0, pl.ds(at, rows), :].reshape(total, cols)

        @pl.when(t < here)
        def _():
            for q in range(group):
                to = rows * ((q + 1) % group)
                plane[to : to + 1, :] += x[q, 0, pl.ds(here * rows + rows + t, 1), :]

        modes[0, t] = dot(table[...], plane[...])
        return carry

    lax.fori_loop(0, here + 1, one, 0)

    def sweep(c, carry):
        cut = pl.ds(pl.multiple_of(c * 8, 8), 8)
        ratio, inverse, low, high = (coef[k, cut, :] for k in range(4))
        square = ratio * ratio
        power = low * ratio
        total_up = jnp.zeros_like(ratio)
        for level in range(here + 1):
            total_up = ratio * total_up + (1.0 + power) * modes[0, level, cut, :]
            power = power * square
        up[0, cut, :] = total_up
        power = high * inverse
        total_down = jnp.zeros_like(ratio)
        for level in range(here, -1, -1):
            total_down = ratio * total_down + (1.0 + power) * modes[0, level, cut, :]
            power = power * square
        down[0, cut, :] = total_down
        return carry

    lax.fori_loop(0, total // 8, sweep, 0)


def backward_kernel(modes, up, down, table, coef, out, phi, *, here, rows, levels):
    group = out.shape[0]
    total, cols = table.shape[0], out.shape[3]

    def sweep(c, carry):
        cut = pl.ds(pl.multiple_of(c * 8, 8), 8)
        ratio, inverse, low, high, scale = (coef[k, cut, :] for k in range(5))
        square = ratio * ratio
        powers_low = []
        powers_high = []
        power = low * ratio
        for level in range(here + 1):
            powers_low.append(1.0 + power)
            power = power * square
        power = high * inverse
        for level in range(here + 1):
            powers_high.append(1.0 + power)
            power = power * square
        powers_high = powers_high[::-1]
        value = up[0, cut, :]
        for level in range(here + 1):
            if level:
                value = ratio * value
            value = value + powers_low[level] * modes[0, level, cut, :]
            phi[level, cut, :] = powers_high[level] * value
        behind = down[0, cut, :]
        for level in range(here, -1, -1):
            phi[level, cut, :] = scale * (phi[level, cut, :] + powers_low[level] * behind)
            behind = ratio * (behind + powers_high[level] * modes[0, level, cut, :])
        return carry

    lax.fori_loop(0, total // 8, sweep, 0)

    first = lax.axis_index("py") * here
    tile = (slice(0, 8), slice(0, 128))
    flat = (lax.broadcasted_iota(jnp.int32, (8, 128), 0) == 0) & (
        lax.broadcasted_iota(jnp.int32, (8, 128), 1) == 0
    )
    below = 0.5 * up[0, 0:8, 0:128]
    whole = below + 0.5 * down[0, 0:8, 0:128]
    for level in range(here + 1):
        whole = whole + modes[0, level, 0:8, 0:128]
    mean = whole * (1.0 / levels)
    value = jnp.zeros((8, 128), jnp.float32)
    for level in range(here + 1):
        phi[level, 0:8, 0:128] = jnp.where(flat, value, phi[level, 0:8, 0:128])
        if level < here:
            below = below + modes[0, level, 0:8, 0:128]
            count = (first + (level + 1)).astype(jnp.float32)
            value = value - (below - count * mean)

    if out.shape[2] > here * rows + rows + here:
        out[:, :, here * rows + rows :, :] = jnp.zeros(
            (group, 1, out.shape[2] - here * rows - rows, cols), jnp.float32
        )

    def one(t, carry):
        at = pl.multiple_of(t * rows, rows)
        field = dot(table[...], phi[t])
        out[:, 0, pl.ds(at, rows), :] = field.reshape(group, rows, cols)

        @pl.when(t < here)
        def _():
            for d in range(group):
                take = rows * ((d + 1) % group)
                out[d, 0, pl.ds(here * rows + rows + t, 1), :] = field[take : take + 1, :]

        return carry

    lax.fori_loop(0, here + 1, one, 0)


def project_kernel(
    x, mult, table, next_mult, next_aux, phi, following, rims, *, levels
):
    t = pl.program_id(0)
    here = pl.num_programs(0)
    problems, rows, cols = phi.shape
    held = rims.shape[1]
    level = lax.axis_index("py") * here + t
    moving = jnp.where(level == levels - 1, 0.0, 1.0)

    def field(at):
        flat = x[:, :, pl.ds(at, rows), :].reshape(problems * rows, cols)
        return dot(flat, table[...]).reshape(problems, rows, cols)

    @pl.when(t == 0)
    def _():
        following[...] = field(0)
        edge = x[:, :, here * rows + rows :, :].reshape(problems * held, cols)
        rims[...] = dot(edge, table[...]).reshape(problems, held, cols)

    phi[...] = following[...]
    following[...] = field(pl.multiple_of((t + 1) * rows, rows))
    row = lax.broadcasted_iota(jnp.int32, (rows, cols), 0)

    def one(b, carry):
        here_phi = phi[b]
        rim = jnp.broadcast_to(rims[b, pl.ds(t, 1), :], (rows, cols))
        grad_time = (following[b] - here_phi) * moving
        grad_first = jnp.where(row == rows - 1, rim, pltpu.roll(here_phi, rows - 1, 0)) - here_phi
        grad_second = pltpu.roll(here_phi, cols - 1, 1) - here_phi
        mult_time, mult_first, mult_second = (mult[k, 0, b] for k in range(3))
        time_part = grad_time + mult_time / PENALTY
        first = grad_first + mult_first / PENALTY
        second = grad_second + mult_second / PENALTY
        kinetic = 0.5 * (first * first + second * second)
        offset_one = 1.0 + time_part
        solid = kinetic > 1e-37
        root = jnp.exp(jnp.log(jnp.where(solid, kinetic, 1.0)) * (1.0 / 3.0))
        scaling = jnp.maximum(offset_one, 1.0) + jnp.where(solid, root, 0.0)
        for newton_step in range(NEWTON):
            residue = scaling * scaling * (scaling - offset_one) - kinetic
            derivative = scaling * (3.0 * scaling - 2.0 * offset_one)
            scaling = jnp.maximum(scaling - residue / derivative, 1.0)
        feasible = time_part + kinetic <= 0.0
        shrink = jnp.where(feasible, 1.0, 1.0 / scaling)
        out_time = jnp.where(feasible, time_part, time_part - (scaling - 1.0))
        out_first = first * shrink
        out_second = second * shrink
        next_aux[0, 0, b] = out_time
        next_aux[1, 0, b] = out_first
        next_aux[2, 0, b] = out_second
        next_mult[0, 0, b] = mult_time + PENALTY * (grad_time - out_time)
        next_mult[1, 0, b] = mult_first + PENALTY * (grad_first - out_first)
        next_mult[2, 0, b] = mult_second + PENALTY * (grad_second - out_second)
        return carry

    lax.fori_loop(0, problems, one, 0)


def params():
    return pltpu.CompilerParams(vmem_limit_bytes=VMEM_LIMIT)


def whole_block(shape):
    return pl.BlockSpec(shape, lambda *_: (0,) * len(shape))


def passed_along(value, steps):
    count = lax.axis_size("py")
    initial, last = (max(0, -steps), min(count, count - steps))
    return lax.ppermute(value, "py", [(k, k + steps) for k in range(initial, last)])


def local(multiplier, auxiliary, density_start, density_end):
    _, here, problems, rows, cols = multiplier.shape
    blocks = lax.axis_size("py")
    levels = here * blocks
    group = lax.axis_size("grp") * lax.axis_size("px")
    per = problems // group
    row_total = rows * group
    held = -(-here // 8) * 8
    packed = here * rows + rows + held
    f32 = jnp.float32
    table_cols = hartley_table(cols)
    table_rows = hartley_table(row_total)
    coef, step = mode_tables(row_total, cols, here, blocks, lax.axis_index("py"))

    level_block = pl.BlockSpec((3, 1, problems, rows, cols), lambda t: (0, t, 0, 0, 0))
    density_block = whole_block((problems, rows, cols))
    payload = pl.pallas_call(
        functools.partial(source_kernel, levels=levels),
        out_shape=jax.ShapeDtypeStruct((group, per, packed, cols), f32),
        grid=(here,),
        in_specs=[level_block, level_block, density_block, density_block, whole_block((cols, cols))],
        out_specs=whole_block((group, per, packed, cols)),
        scratch_shapes=[
            pltpu.VMEM((problems, rows, cols), f32),
            pltpu.VMEM((problems, rows, cols), f32),
            pltpu.VMEM((problems, held, cols), f32),
        ],
        compiler_params=params(),
        name="source",
    )(multiplier, auxiliary, density_start, density_end, table_cols)

    pencil = lax.all_to_all(payload, SPACE, split_axis=0, concat_axis=0, tiled=True)

    pencil_block = pl.BlockSpec((group, 1, packed, cols), lambda b: (0, b, 0, 0))
    modes_block = pl.BlockSpec((1, here + 1, row_total, cols), lambda b: (b, 0, 0, 0))
    carry_block = pl.BlockSpec((1, row_total, cols), lambda b: (b, 0, 0))
    carry_shape = jax.ShapeDtypeStruct((per, row_total, cols), f32)
    modes, up_own, down_own = pl.pallas_call(
        functools.partial(forward_kernel, here=here, rows=rows),
        out_shape=(
            jax.ShapeDtypeStruct((per, here + 1, row_total, cols), f32),
            carry_shape,
            carry_shape,
        ),
        grid=(per,),
        in_specs=[pencil_block, whole_block((row_total, row_total)), whole_block(coef.shape)],
        out_specs=(modes_block, carry_block, carry_block),
        scratch_shapes=[pltpu.VMEM((row_total, cols), f32)],
        compiler_params=params(),
        name="forward",
    )(pencil, table_rows, coef)

    up, down = up_own, down_own
    for hop in range(blocks - 1):
        up_in = passed_along(up, 1)
        down_in = passed_along(down, -1)
        up = up_own + step * up_in
        down = down_own + step * down_in

    returned = pl.pallas_call(
        functools.partial(backward_kernel, here=here, rows=rows, levels=levels),
        out_shape=jax.ShapeDtypeStruct((group, per, packed, cols), f32),
        grid=(per,),
        in_specs=[
            modes_block,
            carry_block,
            carry_block,
            whole_block((row_total, row_total)),
            whole_block(coef.shape),
        ],
        out_specs=pencil_block,
        scratch_shapes=[pltpu.VMEM((here + 1, row_total, cols), f32)],
        compiler_params=params(),
        name="backward",
    )(modes, up_in, down_in, table_rows, coef)

    slab = lax.all_to_all(returned, SPACE, split_axis=0, concat_axis=0, tiled=True)

    out_shape = jax.ShapeDtypeStruct(multiplier.shape, f32)
    return pl.pallas_call(
        functools.partial(project_kernel, levels=levels),
        out_shape=(out_shape, out_shape),
        grid=(here,),
        in_specs=[
            whole_block((group, per, packed, cols)),
            level_block,
            whole_block((cols, cols)),
        ],
        out_specs=(level_block, level_block),
        scratch_shapes=[
            pltpu.VMEM((problems, rows, cols), f32),
            pltpu.VMEM((problems, rows, cols), f32),
            pltpu.VMEM((problems, held, cols), f32),
        ],
        compiler_params=params(),
        name="project",
    )(slab, multiplier, table_cols)


def solution(mesh):
    placed = (
        P(None, "py", None, ("grp", "px"), None),
        P(None, "py", None, ("grp", "px"), None),
        P(None, ("grp", "px"), None),
        P(None, ("grp", "px"), None),
    )
    return jax.shard_map(
        local,
        mesh=mesh,
        in_specs=placed,
        out_specs=(
            P(None, "py", None, ("grp", "px"), None),
            P(None, "py", None, ("grp", "px"), None),
        ),
        check_vma=False,
    )
```

```python
import functools
import math

import jax
import jax.numpy as jnp
from jax import lax
from jax.experimental import pallas as pl
from jax.experimental.pallas import tpu as pltpu
from jax.sharding import PartitionSpec as P

NEWTON = 4
PENALTY = 1.0
PRECISE = lax.Precision.HIGHEST
VMEM_LIMIT = 60 * 1024 * 1024
SPACE = ("grp", "px")


def dot(a, b):
    return jnp.dot(a, b, precision=PRECISE, preferred_element_type=jnp.float32)


def hartley_table(length):
    row_index = lax.broadcasted_iota(jnp.int32, (length, length), 0)
    col_index = lax.broadcasted_iota(jnp.int32, (length, length), 1)
    phase_index = row_index * col_index % length
    angles = phase_index.astype(jnp.float32) * (2.0 * math.pi / length)
    return (jnp.cos(angles) + jnp.sin(angles)) / math.sqrt(length)


def mode_tables(rows, cols, here, blocks, block):
    m = lax.broadcasted_iota(jnp.int32, (rows, cols), 0)
    n = lax.broadcasted_iota(jnp.int32, (rows, cols), 1)
    m = jnp.minimum(m, rows - m).astype(jnp.float32)
    n = jnp.minimum(n, cols - n).astype(jnp.float32)
    lam = 4.0 * jnp.sin(m * (math.pi / rows)) ** 2 + 4.0 * jnp.sin(n * (math.pi / cols)) ** 2
    sinh = jnp.sqrt(lam * (1.0 + 0.25 * lam))
    inverse = 1.0 + 0.5 * lam + sinh
    ratio = 1.0 / inverse
    step = lax.integer_pow(ratio, here)
    double = step * step
    low = jnp.ones_like(step)
    high = jnp.ones_like(step)
    full = double
    for k in range(1, blocks):
        low = jnp.where(block >= k, low * double, low)
        high = jnp.where(blocks - 1 - block >= k, high * double, high)
        full = full * double
    positive = lam > 0.0
    scale = jnp.where(
        positive, 0.5 / jnp.where(positive, sinh * (1.0 - full), 1.0), 0.0
    )
    return jnp.stack([ratio, inverse, low, high, scale]), step


def source_kernel(mult, aux, start, end, table, out, prev, body, tail, *, levels):
    t = pl.program_id(0)
    here = pl.num_programs(0)
    problems, rows, cols = body.shape
    group, per = out.shape[0], out.shape[1]
    level = lax.axis_index("py") * here + t
    first = level == 0
    last = level == levels - 1

    @pl.when(t == 0)
    def _():
        prev[...] = jnp.zeros_like(prev)
        tail[...] = jnp.zeros_like(tail)

    row = lax.broadcasted_iota(jnp.int32, (rows, cols), 0)
    keep = jnp.where(last, 0.0, 1.0)
    begin = jnp.where(first, -1.0 / PENALTY, 0.0)
    finish = jnp.where(last, 1.0 / PENALTY, 0.0)

    def one(b, carry):
        along = aux[1, 0, b] - mult[1, 0, b] / PENALTY
        beside = jnp.where(row == 0, 0.0, pltpu.roll(along, 1, 0))
        second = aux[2, 0, b] - mult[2, 0, b] / PENALTY
        across = pltpu.roll(second, 1, 1) - second
        now = (aux[0, 0, b] - mult[0, 0, b] / PENALTY) * keep
        boundary = begin * start[b] + finish * end[b]
        body[b] = prev[b] - now + beside - along + across + boundary
        prev[b] = now
        tail[b, pl.ds(t, 1), :] = along[rows - 1 :, :]
        return carry

    lax.fori_loop(0, problems, one, 0)
    spread = dot(body[...].reshape(problems * rows, cols), table[...])
    at = pl.multiple_of(t * rows, rows)
    out[:, :, pl.ds(at, rows), :] = spread.reshape(group, per, rows, cols)

    @pl.when(t == here - 1)
    def _():
        beyond = dot(prev[...].reshape(problems * rows, cols), table[...])
        out[:, :, here * rows : here * rows + rows, :] = beyond.reshape(group, per, rows, cols)
        held = tail.shape[1]
        rims = dot(tail[...].reshape(problems * held, cols), table[...])
        out[:, :, here * rows + rows :, :] = rims.reshape(group, per, held, cols)


def forward_kernel(x, table, coef, modes, up, down, plane, *, here, rows):
    group = x.shape[0]
    total, cols = table.shape[0], x.shape[3]

    def one(t, carry):
        at = pl.multiple_of(t * rows, rows)
        plane[...] = x[:, 0, pl.ds(at, rows), :].reshape(total, cols)

        @pl.when(t < here)
        def _():
            for q in range(group):
                to = rows * ((q + 1) % group)
                plane[to : to + 1, :] += x[q, 0, pl.ds(here * rows + rows + t, 1), :]

        modes[0, t] = dot(table[...], plane[...])
        return carry

    lax.fori_loop(0, here + 1, one, 0)

    def sweep(c, carry):
        cut = pl.ds(pl.multiple_of(c * 8, 8), 8)
        ratio, inverse, low, high = (coef[k, cut, :] for k in range(4))
        square = ratio * ratio
        power = low * ratio
        total_up = jnp.zeros_like(ratio)
        for level in range(here + 1):
            total_up = ratio * total_up + (1.0 + power) * modes[0, level, cut, :]
            power = power * square
        up[0, cut, :] = total_up
        power = high * inverse
        total_down = jnp.zeros_like(ratio)
        for level in range(here, -1, -1):
            total_down = ratio * total_down + (1.0 + power) * modes[0, level, cut, :]
            power = power * square
        down[0, cut, :] = total_down
        return carry

    lax.fori_loop(0, total // 8, sweep, 0)


def carry_kernel(up_own, down_own, step, up_in, down_in, up_got, down_got, up_out, down_out,
                 up_sent, up_came, down_sent, down_came, *, blocks, pieces, lag):
    me = lax.axis_index("py")
    size = up_own.shape[1] // pieces
    has_lower = me > 0
    has_upper = me < blocks - 1
    pairs = [(b, c) for b in range(up_own.shape[0]) for c in range(pieces)]

    def copy(source, target, sent, came, k, other):
        b, c = pairs[k]
        cut = pl.ds(c * size, size)
        return pltpu.make_async_remote_copy(
            src_ref=source.at[b, cut, :],
            dst_ref=target.at[b, cut, :],
            send_sem=sent.at[k],
            recv_sem=came.at[k],
            device_id={"py": other},
            device_id_type=pl.DeviceIdType.MESH,
        )

    barrier = pltpu.get_barrier_semaphore()

    @pl.when(has_lower)
    def _():
        pl.semaphore_signal(
            barrier, inc=1, device_id={"py": me - 1}, device_id_type=pl.DeviceIdType.MESH
        )

    @pl.when(has_upper)
    def _():
        pl.semaphore_signal(
            barrier, inc=1, device_id={"py": me + 1}, device_id_type=pl.DeviceIdType.MESH
        )

    @pl.when(has_lower & has_upper)
    def _():
        pl.semaphore_wait(barrier, 2)

    @pl.when(jnp.logical_not(has_lower & has_upper))
    def _():
        pl.semaphore_wait(barrier, 1)

    def relay(k, own, got, out, sent, came, first, last, ahead):
        b, c = pairs[k]
        cut = pl.ds(c * size, size)

        @pl.when(jnp.logical_not(first))
        def _():
            copy(out, got, sent, came, k, ahead).wait_recv()

            @pl.when(jnp.logical_not(last))
            def _():
                out[b, cut, :] = own[b, cut, :] + step[cut, :] * got[b, cut, :]
                copy(out, got, sent, came, k, ahead).start()

    up = (up_own, up_got, up_out, up_sent, up_came, me == 0, me == blocks - 1,
          (me + 1) % blocks)
    down = (down_own, down_got, down_out, down_sent, down_came, me == blocks - 1, me == 0,
            (me + blocks - 1) % blocks)

    @pl.when(me == 0)
    def _():
        for k in range(len(pairs)):
            copy(up_own, up_got, up_sent, up_came, k, me + 1).start()

    @pl.when(me == blocks - 1)
    def _():
        for k in range(len(pairs)):
            copy(down_own, down_got, down_sent, down_came, k, me - 1).start()

    def weave(early, late):
        for k in range(len(pairs) + lag):
            if k < len(pairs):
                relay(k, *early)
            if k >= lag:
                relay(k - lag, *late)

    lower_half = me < blocks // 2

    @pl.when(lower_half)
    def _():
        weave(up, down)

    @pl.when(jnp.logical_not(lower_half))
    def _():
        weave(down, up)

    @pl.when(has_lower)
    def _():
        up_in[...] = up_got[...]
        for k in range(len(pairs)):
            copy(down_out, down_got, down_sent, down_came, k, me - 1).wait_send()

    @pl.when(me == 0)
    def _():
        up_in[...] = jnp.zeros_like(up_in)

    @pl.when(has_upper)
    def _():
        down_in[...] = down_got[...]
        for k in range(len(pairs)):
            copy(up_out, up_got, up_sent, up_came, k, me + 1).wait_send()

    @pl.when(me == blocks - 1)
    def _():
        down_in[...] = jnp.zeros_like(down_in)


def backward_kernel(modes, up, down, table, coef, out, phi, *, here, rows, levels):
    group = out.shape[0]
    total, cols = table.shape[0], out.shape[3]

    def sweep(c, carry):
        cut = pl.ds(pl.multiple_of(c * 8, 8), 8)
        ratio, inverse, low, high, scale = (coef[k, cut, :] for k in range(5))
        square = ratio * ratio
        powers_low = []
        powers_high = []
        power = low * ratio
        for level in range(here + 1):
            powers_low.append(1.0 + power)
            power = power * square
        power = high * inverse
        for level in range(here + 1):
            powers_high.append(1.0 + power)
            power = power * square
        powers_high = powers_high[::-1]
        value = up[0, cut, :]
        for level in range(here + 1):
            if level:
                value = ratio * value
            value = value + powers_low[level] * modes[0, level, cut, :]
            phi[level, cut, :] = powers_high[level] * value
        behind = down[0, cut, :]
        for level in range(here, -1, -1):
            phi[level, cut, :] = scale * (phi[level, cut, :] + powers_low[level] * behind)
            behind = ratio * (behind + powers_high[level] * modes[0, level, cut, :])
        return carry

    lax.fori_loop(0, total // 8, sweep, 0)

    first = lax.axis_index("py") * here
    tile = (slice(0, 8), slice(0, 128))
    flat = (lax.broadcasted_iota(jnp.int32, (8, 128), 0) == 0) & (
        lax.broadcasted_iota(jnp.int32, (8, 128), 1) == 0
    )
    below = 0.5 * up[0, 0:8, 0:128]
    whole = below + 0.5 * down[0, 0:8, 0:128]
    for level in range(here + 1):
        whole = whole + modes[0, level, 0:8, 0:128]
    mean = whole * (1.0 / levels)
    value = jnp.zeros((8, 128), jnp.float32)
    for level in range(here + 1):
        phi[level, 0:8, 0:128] = jnp.where(flat, value, phi[level, 0:8, 0:128])
        if level < here:
            below = below + modes[0, level, 0:8, 0:128]
            count = (first + (level + 1)).astype(jnp.float32)
            value = value - (below - count * mean)

    if out.shape[2] > here * rows + rows + here:
        out[:, :, here * rows + rows :, :] = jnp.zeros(
            (group, 1, out.shape[2] - here * rows - rows, cols), jnp.float32
        )

    def one(t, carry):
        at = pl.multiple_of(t * rows, rows)
        field = dot(table[...], phi[t])
        out[:, 0, pl.ds(at, rows), :] = field.reshape(group, rows, cols)

        @pl.when(t < here)
        def _():
            for d in range(group):
                take = rows * ((d + 1) % group)
                out[d, 0, pl.ds(here * rows + rows + t, 1), :] = field[take : take + 1, :]

        return carry

    lax.fori_loop(0, here + 1, one, 0)


def project_kernel(
    x, mult, table, next_mult, next_aux, phi, following, rims, *, levels
):
    t = pl.program_id(0)
    here = pl.num_programs(0)
    problems, rows, cols = phi.shape
    held = rims.shape[1]
    level = lax.axis_index("py") * here + t
    moving = jnp.where(level == levels - 1, 0.0, 1.0)

    def field(at):
        flat = x[:, :, pl.ds(at, rows), :].reshape(problems * rows, cols)
        return dot(flat, table[...]).reshape(problems, rows, cols)

    @pl.when(t == 0)
    def _():
        following[...] = field(0)
        edge = x[:, :, here * rows + rows :, :].reshape(problems * held, cols)
        rims[...] = dot(edge, table[...]).reshape(problems, held, cols)

    phi[...] = following[...]
    following[...] = field(pl.multiple_of((t + 1) * rows, rows))
    row = lax.broadcasted_iota(jnp.int32, (rows, cols), 0)

    def one(b, carry):
        here_phi = phi[b]
        rim = jnp.broadcast_to(rims[b, pl.ds(t, 1), :], (rows, cols))
        grad_time = (following[b] - here_phi) * moving
        grad_first = jnp.where(row == rows - 1, rim, pltpu.roll(here_phi, rows - 1, 0)) - here_phi
        grad_second = pltpu.roll(here_phi, cols - 1, 1) - here_phi
        mult_time, mult_first, mult_second = (mult[k, 0, b] for k in range(3))
        time_part = grad_time + mult_time / PENALTY
        first = grad_first + mult_first / PENALTY
        second = grad_second + mult_second / PENALTY
        kinetic = 0.5 * (first * first + second * second)
        offset_one = 1.0 + time_part
        solid = kinetic > 1e-37
        root = jnp.exp(jnp.log(jnp.where(solid, kinetic, 1.0)) * (1.0 / 3.0))
        scaling = jnp.maximum(offset_one, 1.0) + jnp.where(solid, root, 0.0)
        for newton_step in range(NEWTON):
            residue = scaling * scaling * (scaling - offset_one) - kinetic
            derivative = scaling * (3.0 * scaling - 2.0 * offset_one)
            scaling = jnp.maximum(scaling - residue / derivative, 1.0)
        feasible = time_part + kinetic <= 0.0
        shrink = jnp.where(feasible, 1.0, 1.0 / scaling)
        out_time = jnp.where(feasible, time_part, time_part - (scaling - 1.0))
        out_first = first * shrink
        out_second = second * shrink
        next_aux[0, 0, b] = out_time
        next_aux[1, 0, b] = out_first
        next_aux[2, 0, b] = out_second
        next_mult[0, 0, b] = mult_time + PENALTY * (grad_time - out_time)
        next_mult[1, 0, b] = mult_first + PENALTY * (grad_first - out_first)
        next_mult[2, 0, b] = mult_second + PENALTY * (grad_second - out_second)
        return carry

    lax.fori_loop(0, problems, one, 0)


def params():
    return pltpu.CompilerParams(vmem_limit_bytes=VMEM_LIMIT)


def whole_block(shape):
    return pl.BlockSpec(shape, lambda *_: (0,) * len(shape))


def local(multiplier, auxiliary, density_start, density_end):
    _, here, problems, rows, cols = multiplier.shape
    blocks = lax.axis_size("py")
    levels = here * blocks
    group = lax.axis_size("grp") * lax.axis_size("px")
    per = problems // group
    row_total = rows * group
    held = -(-here // 8) * 8
    packed = here * rows + rows + held
    f32 = jnp.float32
    table_cols = hartley_table(cols)
    table_rows = hartley_table(row_total)
    coef, step = mode_tables(row_total, cols, here, blocks, lax.axis_index("py"))

    level_block = pl.BlockSpec((3, 1, problems, rows, cols), lambda t: (0, t, 0, 0, 0))
    density_block = whole_block((problems, rows, cols))
    payload = pl.pallas_call(
        functools.partial(source_kernel, levels=levels),
        out_shape=jax.ShapeDtypeStruct((group, per, packed, cols), f32),
        grid=(here,),
        in_specs=[level_block, level_block, density_block, density_block, whole_block((cols, cols))],
        out_specs=whole_block((group, per, packed, cols)),
        scratch_shapes=[
            pltpu.VMEM((problems, rows, cols), f32),
            pltpu.VMEM((problems, rows, cols), f32),
            pltpu.VMEM((problems, held, cols), f32),
        ],
        compiler_params=params(),
        name="source",
    )(multiplier, auxiliary, density_start, density_end, table_cols)

    pencil = lax.all_to_all(payload, SPACE, split_axis=0, concat_axis=0, tiled=True)

    pencil_block = pl.BlockSpec((group, 1, packed, cols), lambda b: (0, b, 0, 0))
    modes_block = pl.BlockSpec((1, here + 1, row_total, cols), lambda b: (b, 0, 0, 0))
    carry_block = pl.BlockSpec((1, row_total, cols), lambda b: (b, 0, 0))
    carry_shape = jax.ShapeDtypeStruct((per, row_total, cols), f32)
    modes, up_own, down_own = pl.pallas_call(
        functools.partial(forward_kernel, here=here, rows=rows),
        out_shape=(
            jax.ShapeDtypeStruct((per, here + 1, row_total, cols), f32),
            carry_shape,
            carry_shape,
        ),
        grid=(per,),
        in_specs=[pencil_block, whole_block((row_total, row_total)), whole_block(coef.shape)],
        out_specs=(modes_block, carry_block, carry_block),
        scratch_shapes=[pltpu.VMEM((row_total, cols), f32)],
        compiler_params=params(),
        name="forward",
    )(pencil, table_rows, coef)

    pieces = math.gcd(row_total // 8, 4)
    count = per * pieces
    vmem = pl.BlockSpec(memory_space=pltpu.VMEM)
    up_in, down_in = pl.pallas_call(
        functools.partial(carry_kernel, blocks=blocks, pieces=pieces, lag=min(3, count)),
        out_shape=(carry_shape, carry_shape),
        in_specs=[vmem, vmem, vmem],
        out_specs=(vmem, vmem),
        scratch_shapes=[pltpu.VMEM((per, row_total, cols), f32)] * 4
        + [pltpu.SemaphoreType.DMA((count,))] * 4,
        compiler_params=pltpu.CompilerParams(
            collective_id=0, has_side_effects=True, vmem_limit_bytes=24 * 1024 * 1024
        ),
        name="carry",
    )(up_own, down_own, step)

    returned = pl.pallas_call(
        functools.partial(backward_kernel, here=here, rows=rows, levels=levels),
        out_shape=jax.ShapeDtypeStruct((group, per, packed, cols), f32),
        grid=(per,),
        in_specs=[
            modes_block,
            carry_block,
            carry_block,
            whole_block((row_total, row_total)),
            whole_block(coef.shape),
        ],
        out_specs=pencil_block,
        scratch_shapes=[pltpu.VMEM((here + 1, row_total, cols), f32)],
        compiler_params=params(),
        name="backward",
    )(modes, up_in, down_in, table_rows, coef)

    slab = lax.all_to_all(returned, SPACE, split_axis=0, concat_axis=0, tiled=True)

    out_shape = jax.ShapeDtypeStruct(multiplier.shape, f32)
    return pl.pallas_call(
        functools.partial(project_kernel, levels=levels),
        out_shape=(out_shape, out_shape),
        grid=(here,),
        in_specs=[
            whole_block((group, per, packed, cols)),
            level_block,
            whole_block((cols, cols)),
        ],
        out_specs=(level_block, level_block),
        scratch_shapes=[
            pltpu.VMEM((problems, rows, cols), f32),
            pltpu.VMEM((problems, rows, cols), f32),
            pltpu.VMEM((problems, held, cols), f32),
        ],
        compiler_params=params(),
        name="project",
    )(slab, multiplier, table_cols)


def solution(mesh):
    placed = (
        P(None, "py", None, ("grp", "px"), None),
        P(None, "py", None, ("grp", "px"), None),
        P(None, ("grp", "px"), None),
        P(None, ("grp", "px"), None),
    )
    return jax.shard_map(
        local,
        mesh=mesh,
        in_specs=placed,
        out_specs=(
            P(None, "py", None, ("grp", "px"), None),
            P(None, "py", None, ("grp", "px"), None),
        ),
        check_vma=False,
    )
```

```python
import functools
import math

import jax
import jax.numpy as jnp
from jax import lax
from jax.experimental import pallas as pl
from jax.experimental.pallas import tpu as pltpu
from jax.sharding import PartitionSpec as P

NEWTON = 4
PENALTY = 1.0
PRECISE = lax.Precision.HIGHEST
VMEM_LIMIT = 60 * 1024 * 1024
SPACE = ("grp", "px")


def dot(a, b):
    return jnp.dot(a, b, precision=PRECISE, preferred_element_type=jnp.float32)


def hartley_table(length):
    row_index = lax.broadcasted_iota(jnp.int32, (length, length), 0)
    col_index = lax.broadcasted_iota(jnp.int32, (length, length), 1)
    phase_index = row_index * col_index % length
    angles = phase_index.astype(jnp.float32) * (2.0 * math.pi / length)
    return (jnp.cos(angles) + jnp.sin(angles)) / math.sqrt(length)


def mode_tables(rows, cols, here, blocks, block):
    m = lax.broadcasted_iota(jnp.int32, (rows, cols), 0)
    n = lax.broadcasted_iota(jnp.int32, (rows, cols), 1)
    m = jnp.minimum(m, rows - m).astype(jnp.float32)
    n = jnp.minimum(n, cols - n).astype(jnp.float32)
    lam = 4.0 * jnp.sin(m * (math.pi / rows)) ** 2 + 4.0 * jnp.sin(n * (math.pi / cols)) ** 2
    sinh = jnp.sqrt(lam * (1.0 + 0.25 * lam))
    inverse = 1.0 + 0.5 * lam + sinh
    ratio = 1.0 / inverse
    step = lax.integer_pow(ratio, here)
    double = step * step
    low = jnp.ones_like(step)
    high = jnp.ones_like(step)
    full = double
    for k in range(1, blocks):
        low = jnp.where(block >= k, low * double, low)
        high = jnp.where(blocks - 1 - block >= k, high * double, high)
        full = full * double
    positive = lam > 0.0
    scale = jnp.where(
        positive, 0.5 / jnp.where(positive, sinh * (1.0 - full), 1.0), 0.0
    )
    return jnp.stack([ratio, inverse, low, high, scale]), step


def source_kernel(mult, aux, start, end, table, out, prev, body, tail, *, levels):
    t = pl.program_id(0)
    here = pl.num_programs(0)
    problems, rows, cols = body.shape
    group, per = out.shape[0], out.shape[1]
    level = lax.axis_index("py") * here + t
    first = level == 0
    last = level == levels - 1

    @pl.when(t == 0)
    def _():
        prev[...] = jnp.zeros_like(prev)
        tail[...] = jnp.zeros_like(tail)

    row = lax.broadcasted_iota(jnp.int32, (rows, cols), 0)
    keep = jnp.where(last, 0.0, 1.0)
    begin = jnp.where(first, -1.0 / PENALTY, 0.0)
    finish = jnp.where(last, 1.0 / PENALTY, 0.0)

    def one(b, carry):
        along = aux[1, 0, b] - mult[1, 0, b] / PENALTY
        beside = jnp.where(row == 0, 0.0, pltpu.roll(along, 1, 0))
        second = aux[2, 0, b] - mult[2, 0, b] / PENALTY
        across = pltpu.roll(second, 1, 1) - second
        now = (aux[0, 0, b] - mult[0, 0, b] / PENALTY) * keep
        boundary = begin * start[b] + finish * end[b]
        body[b] = prev[b] - now + beside - along + across + boundary
        prev[b] = now
        tail[b, pl.ds(t, 1), :] = along[rows - 1 :, :]
        return carry

    lax.fori_loop(0, problems, one, 0, unroll=4)
    spread = dot(body[...].reshape(problems * rows, cols), table[...])
    at = pl.multiple_of(t * rows, rows)
    out[:, :, pl.ds(at, rows), :] = spread.reshape(group, per, rows, cols)

    @pl.when(t == here - 1)
    def _():
        beyond = dot(prev[...].reshape(problems * rows, cols), table[...])
        out[:, :, here * rows : here * rows + rows, :] = beyond.reshape(group, per, rows, cols)
        held = tail.shape[1]
        rims = dot(tail[...].reshape(problems * held, cols), table[...])
        out[:, :, here * rows + rows :, :] = rims.reshape(group, per, held, cols)


def forward_kernel(x, table, coef, modes, up, down, plane, *, here, rows):
    group = x.shape[0]
    total, cols = table.shape[0], x.shape[3]

    def one(t, carry):
        at = pl.multiple_of(t * rows, rows)
        plane[...] = x[:, 0, pl.ds(at, rows), :].reshape(total, cols)

        @pl.when(t < here)
        def _():
            for q in range(group):
                to = rows * ((q + 1) % group)
                plane[to : to + 1, :] += x[q, 0, pl.ds(here * rows + rows + t, 1), :]

        modes[0, t] = dot(table[...], plane[...])
        return carry

    lax.fori_loop(0, here + 1, one, 0)

    def sweep(c, carry):
        cut = pl.ds(pl.multiple_of(c * 8, 8), 8)
        ratio, inverse, low, high = (coef[k, cut, :] for k in range(4))
        square = ratio * ratio
        power = low * ratio
        total_up = jnp.zeros_like(ratio)
        for level in range(here + 1):
            total_up = ratio * total_up + (1.0 + power) * modes[0, level, cut, :]
            power = power * square
        up[0, cut, :] = total_up
        power = high * inverse
        total_down = jnp.zeros_like(ratio)
        for level in range(here, -1, -1):
            total_down = ratio * total_down + (1.0 + power) * modes[0, level, cut, :]
            power = power * square
        down[0, cut, :] = total_down
        return carry

    lax.fori_loop(0, total // 8, sweep, 0, unroll=4)


def carry_kernel(up_own, down_own, step, up_in, down_in, up_got, down_got, up_out, down_out,
                 up_sent, up_came, down_sent, down_came, *, blocks, pieces, lag):
    me = lax.axis_index("py")
    size = up_own.shape[1] // pieces
    has_lower = me > 0
    has_upper = me < blocks - 1
    pairs = [(b, c) for b in range(up_own.shape[0]) for c in range(pieces)]

    def copy(source, target, sent, came, k, other):
        b, c = pairs[k]
        cut = pl.ds(c * size, size)
        return pltpu.make_async_remote_copy(
            src_ref=source.at[b, cut, :],
            dst_ref=target.at[b, cut, :],
            send_sem=sent.at[k],
            recv_sem=came.at[k],
            device_id={"py": other},
            device_id_type=pl.DeviceIdType.MESH,
        )

    barrier = pltpu.get_barrier_semaphore()

    @pl.when(has_lower)
    def _():
        pl.semaphore_signal(
            barrier, inc=1, device_id={"py": me - 1}, device_id_type=pl.DeviceIdType.MESH
        )

    @pl.when(has_upper)
    def _():
        pl.semaphore_signal(
            barrier, inc=1, device_id={"py": me + 1}, device_id_type=pl.DeviceIdType.MESH
        )

    @pl.when(has_lower & has_upper)
    def _():
        pl.semaphore_wait(barrier, 2)

    @pl.when(jnp.logical_not(has_lower & has_upper))
    def _():
        pl.semaphore_wait(barrier, 1)

    def relay(k, own, got, out, sent, came, first, last, ahead):
        b, c = pairs[k]
        cut = pl.ds(c * size, size)

        @pl.when(jnp.logical_not(first))
        def _():
            copy(out, got, sent, came, k, ahead).wait_recv()

            @pl.when(jnp.logical_not(last))
            def _():
                out[b, cut, :] = own[b, cut, :] + step[cut, :] * got[b, cut, :]
                copy(out, got, sent, came, k, ahead).start()

    up = (up_own, up_got, up_out, up_sent, up_came, me == 0, me == blocks - 1,
          (me + 1) % blocks)
    down = (down_own, down_got, down_out, down_sent, down_came, me == blocks - 1, me == 0,
            (me + blocks - 1) % blocks)

    @pl.when(me == 0)
    def _():
        for k in range(len(pairs)):
            copy(up_own, up_got, up_sent, up_came, k, me + 1).start()

    @pl.when(me == blocks - 1)
    def _():
        for k in range(len(pairs)):
            copy(down_own, down_got, down_sent, down_came, k, me - 1).start()

    def weave(early, late):
        for k in range(len(pairs) + lag):
            if k < len(pairs):
                relay(k, *early)
            if k >= lag:
                relay(k - lag, *late)

    lower_half = me < blocks // 2

    @pl.when(lower_half)
    def _():
        weave(up, down)

    @pl.when(jnp.logical_not(lower_half))
    def _():
        weave(down, up)

    @pl.when(has_lower)
    def _():
        up_in[...] = up_got[...]
        for k in range(len(pairs)):
            copy(down_out, down_got, down_sent, down_came, k, me - 1).wait_send()

    @pl.when(me == 0)
    def _():
        up_in[...] = jnp.zeros_like(up_in)

    @pl.when(has_upper)
    def _():
        down_in[...] = down_got[...]
        for k in range(len(pairs)):
            copy(up_out, up_got, up_sent, up_came, k, me + 1).wait_send()

    @pl.when(me == blocks - 1)
    def _():
        down_in[...] = jnp.zeros_like(down_in)


def backward_kernel(modes, up, down, table, coef, out, phi, *, here, rows, levels):
    group = out.shape[0]
    total, cols = table.shape[0], out.shape[3]

    def sweep(c, carry):
        cut = pl.ds(pl.multiple_of(c * 8, 8), 8)
        ratio, inverse, low, high, scale = (coef[k, cut, :] for k in range(5))
        square = ratio * ratio
        powers_low = []
        powers_high = []
        power = low * ratio
        for level in range(here + 1):
            powers_low.append(1.0 + power)
            power = power * square
        power = high * inverse
        for level in range(here + 1):
            powers_high.append(1.0 + power)
            power = power * square
        powers_high = powers_high[::-1]
        value = up[0, cut, :]
        for level in range(here + 1):
            if level:
                value = ratio * value
            value = value + powers_low[level] * modes[0, level, cut, :]
            phi[level, cut, :] = powers_high[level] * value
        behind = down[0, cut, :]
        for level in range(here, -1, -1):
            phi[level, cut, :] = scale * (phi[level, cut, :] + powers_low[level] * behind)
            behind = ratio * (behind + powers_high[level] * modes[0, level, cut, :])
        return carry

    lax.fori_loop(0, total // 8, sweep, 0, unroll=4)

    first = lax.axis_index("py") * here
    tile = (slice(0, 8), slice(0, 128))
    flat = (lax.broadcasted_iota(jnp.int32, (8, 128), 0) == 0) & (
        lax.broadcasted_iota(jnp.int32, (8, 128), 1) == 0
    )
    below = 0.5 * up[0, 0:8, 0:128]
    whole = below + 0.5 * down[0, 0:8, 0:128]
    for level in range(here + 1):
        whole = whole + modes[0, level, 0:8, 0:128]
    mean = whole * (1.0 / levels)
    value = jnp.zeros((8, 128), jnp.float32)
    for level in range(here + 1):
        phi[level, 0:8, 0:128] = jnp.where(flat, value, phi[level, 0:8, 0:128])
        if level < here:
            below = below + modes[0, level, 0:8, 0:128]
            count = (first + (level + 1)).astype(jnp.float32)
            value = value - (below - count * mean)

    if out.shape[2] > here * rows + rows + here:
        out[:, :, here * rows + rows :, :] = jnp.zeros(
            (group, 1, out.shape[2] - here * rows - rows, cols), jnp.float32
        )

    def one(t, carry):
        at = pl.multiple_of(t * rows, rows)
        field = dot(table[...], phi[t])
        out[:, 0, pl.ds(at, rows), :] = field.reshape(group, rows, cols)

        @pl.when(t < here)
        def _():
            for d in range(group):
                take = rows * ((d + 1) % group)
                out[d, 0, pl.ds(here * rows + rows + t, 1), :] = field[take : take + 1, :]

        return carry

    lax.fori_loop(0, here + 1, one, 0)


def project_kernel(
    x, mult, table, next_mult, next_aux, phi, following, rims, *, levels
):
    t = pl.program_id(0)
    here = pl.num_programs(0)
    problems, rows, cols = phi.shape
    held = rims.shape[1]
    level = lax.axis_index("py") * here + t
    moving = jnp.where(level == levels - 1, 0.0, 1.0)

    def field(at):
        flat = x[:, :, pl.ds(at, rows), :].reshape(problems * rows, cols)
        return dot(flat, table[...]).reshape(problems, rows, cols)

    @pl.when(t == 0)
    def _():
        following[...] = field(0)
        edge = x[:, :, here * rows + rows :, :].reshape(problems * held, cols)
        rims[...] = dot(edge, table[...]).reshape(problems, held, cols)

    phi[...] = following[...]
    following[...] = field(pl.multiple_of((t + 1) * rows, rows))
    row = lax.broadcasted_iota(jnp.int32, (rows, cols), 0)

    def one(b, carry):
        here_phi = phi[b]
        rim = jnp.broadcast_to(rims[b, pl.ds(t, 1), :], (rows, cols))
        grad_time = (following[b] - here_phi) * moving
        grad_first = jnp.where(row == rows - 1, rim, pltpu.roll(here_phi, rows - 1, 0)) - here_phi
        grad_second = pltpu.roll(here_phi, cols - 1, 1) - here_phi
        mult_time, mult_first, mult_second = (mult[k, 0, b] for k in range(3))
        time_part = grad_time + mult_time / PENALTY
        first = grad_first + mult_first / PENALTY
        second = grad_second + mult_second / PENALTY
        kinetic = 0.5 * (first * first + second * second)
        offset_one = 1.0 + time_part
        solid = kinetic > 1e-37
        root = jnp.exp(jnp.log(jnp.where(solid, kinetic, 1.0)) * (1.0 / 3.0))
        scaling = jnp.maximum(offset_one, 1.0) + jnp.where(solid, root, 0.0)
        for newton_step in range(NEWTON):
            residue = scaling * scaling * (scaling - offset_one) - kinetic
            derivative = scaling * (3.0 * scaling - 2.0 * offset_one)
            scaling = jnp.maximum(scaling - residue / derivative, 1.0)
        feasible = time_part + kinetic <= 0.0
        shrink = jnp.where(feasible, 1.0, 1.0 / scaling)
        out_time = jnp.where(feasible, time_part, time_part - (scaling - 1.0))
        out_first = first * shrink
        out_second = second * shrink
        next_aux[0, 0, b] = out_time
        next_aux[1, 0, b] = out_first
        next_aux[2, 0, b] = out_second
        next_mult[0, 0, b] = mult_time + PENALTY * (grad_time - out_time)
        next_mult[1, 0, b] = mult_first + PENALTY * (grad_first - out_first)
        next_mult[2, 0, b] = mult_second + PENALTY * (grad_second - out_second)
        return carry

    lax.fori_loop(0, problems, one, 0, unroll=2)


def params():
    return pltpu.CompilerParams(vmem_limit_bytes=VMEM_LIMIT)


def whole_block(shape):
    return pl.BlockSpec(shape, lambda *_: (0,) * len(shape))


def local(multiplier, auxiliary, density_start, density_end):
    _, here, problems, rows, cols = multiplier.shape
    blocks = lax.axis_size("py")
    levels = here * blocks
    group = lax.axis_size("grp") * lax.axis_size("px")
    per = problems // group
    row_total = rows * group
    held = -(-here // 8) * 8
    packed = here * rows + rows + held
    f32 = jnp.float32
    table_cols = hartley_table(cols)
    table_rows = hartley_table(row_total)
    coef, step = mode_tables(row_total, cols, here, blocks, lax.axis_index("py"))

    level_block = pl.BlockSpec((3, 1, problems, rows, cols), lambda t: (0, t, 0, 0, 0))
    density_block = whole_block((problems, rows, cols))
    payload = pl.pallas_call(
        functools.partial(source_kernel, levels=levels),
        out_shape=jax.ShapeDtypeStruct((group, per, packed, cols), f32),
        grid=(here,),
        in_specs=[level_block, level_block, density_block, density_block, whole_block((cols, cols))],
        out_specs=whole_block((group, per, packed, cols)),
        scratch_shapes=[
            pltpu.VMEM((problems, rows, cols), f32),
            pltpu.VMEM((problems, rows, cols), f32),
            pltpu.VMEM((problems, held, cols), f32),
        ],
        compiler_params=params(),
        name="source",
    )(multiplier, auxiliary, density_start, density_end, table_cols)

    pencil = lax.all_to_all(payload, SPACE, split_axis=0, concat_axis=0, tiled=True)

    pencil_block = pl.BlockSpec((group, 1, packed, cols), lambda b: (0, b, 0, 0))
    modes_block = pl.BlockSpec((1, here + 1, row_total, cols), lambda b: (b, 0, 0, 0))
    carry_block = pl.BlockSpec((1, row_total, cols), lambda b: (b, 0, 0))
    carry_shape = jax.ShapeDtypeStruct((per, row_total, cols), f32)
    modes, up_own, down_own = pl.pallas_call(
        functools.partial(forward_kernel, here=here, rows=rows),
        out_shape=(
            jax.ShapeDtypeStruct((per, here + 1, row_total, cols), f32),
            carry_shape,
            carry_shape,
        ),
        grid=(per,),
        in_specs=[pencil_block, whole_block((row_total, row_total)), whole_block(coef.shape)],
        out_specs=(modes_block, carry_block, carry_block),
        scratch_shapes=[pltpu.VMEM((row_total, cols), f32)],
        compiler_params=params(),
        name="forward",
    )(pencil, table_rows, coef)

    pieces = math.gcd(row_total // 8, 4)
    count = per * pieces
    vmem = pl.BlockSpec(memory_space=pltpu.VMEM)
    up_in, down_in = pl.pallas_call(
        functools.partial(carry_kernel, blocks=blocks, pieces=pieces, lag=min(3, count)),
        out_shape=(carry_shape, carry_shape),
        in_specs=[vmem, vmem, vmem],
        out_specs=(vmem, vmem),
        scratch_shapes=[pltpu.VMEM((per, row_total, cols), f32)] * 4
        + [pltpu.SemaphoreType.DMA((count,))] * 4,
        compiler_params=pltpu.CompilerParams(
            collective_id=0, has_side_effects=True, vmem_limit_bytes=24 * 1024 * 1024
        ),
        name="carry",
    )(up_own, down_own, step)

    returned = pl.pallas_call(
        functools.partial(backward_kernel, here=here, rows=rows, levels=levels),
        out_shape=jax.ShapeDtypeStruct((group, per, packed, cols), f32),
        grid=(per,),
        in_specs=[
            modes_block,
            carry_block,
            carry_block,
            whole_block((row_total, row_total)),
            whole_block(coef.shape),
        ],
        out_specs=pencil_block,
        scratch_shapes=[pltpu.VMEM((here + 1, row_total, cols), f32)],
        compiler_params=params(),
        name="backward",
    )(modes, up_in, down_in, table_rows, coef)

    slab = lax.all_to_all(returned, SPACE, split_axis=0, concat_axis=0, tiled=True)

    out_shape = jax.ShapeDtypeStruct(multiplier.shape, f32)
    return pl.pallas_call(
        functools.partial(project_kernel, levels=levels),
        out_shape=(out_shape, out_shape),
        grid=(here,),
        in_specs=[
            whole_block((group, per, packed, cols)),
            level_block,
            whole_block((cols, cols)),
        ],
        out_specs=(level_block, level_block),
        scratch_shapes=[
            pltpu.VMEM((problems, rows, cols), f32),
            pltpu.VMEM((problems, rows, cols), f32),
            pltpu.VMEM((problems, held, cols), f32),
        ],
        compiler_params=params(),
        name="project",
    )(slab, multiplier, table_cols)


def solution(mesh):
    placed = (
        P(None, "py", None, ("grp", "px"), None),
        P(None, "py", None, ("grp", "px"), None),
        P(None, ("grp", "px"), None),
        P(None, ("grp", "px"), None),
    )
    return jax.shard_map(
        local,
        mesh=mesh,
        in_specs=placed,
        out_specs=(
            P(None, "py", None, ("grp", "px"), None),
            P(None, "py", None, ("grp", "px"), None),
        ),
        check_vma=False,
    )
```
